32 devices in a mesh: groups: 2 (over y), atoms: 8 (over z, x), samples: 2 (over core).
Axes of the slice: x: 2, y: 2, z: 4, core: 2. Of those that a mesh axis runs over, the one named last changes fastest.
Arguments:
- act: bfloat16 [16, 10240, 128], P('samples', ('groups', 'atoms')), parts along dimension 1, may hold values from -6 to 6
- grad_out: bfloat16 [16, 10240, 128], P('samples', ('groups', 'atoms')), parts along dimension 1, may hold values from -6 to 6
- pair: bfloat16 [320, 32, 16, 128], P(('groups', 'atoms')), parts along dimension 0, may hold values from -500 to 500
- w_query: bfloat16 [128, 128], replicated, may hold values from -0.5 to 0.5
- w_key: bfloat16 [128, 128], replicated, may hold values from -0.5 to 0.5
- w_value: bfloat16 [128, 128], replicated, may hold values from -0.5 to 0.5
- w_gate: bfloat16 [128, 128], replicated, may hold values from -0.5 to 0.5
- w_out: bfloat16 [128, 128], replicated, may hold values from -0.5 to 0.5
- w_pair: bfloat16 [16, 4], replicated, may hold values from -1.5 to 1.5
- w_token: float32 [4], replicated, may hold values from -2 to 2
- offsets: int32 [320], P(('groups', 'atoms')), parts along dimension 0, may hold values from -128 to 32, as said below
- atom_token: int32 [10240], P(('groups', 'atoms')), parts along dimension 0, may hold values from 0 to 639, never falling along the last dimension, each value on 1 to 24 neighbouring positions
- padding: int32 [16], P(('groups', 'atoms')), parts along dimension 0, may hold values from 0 to 64, as said below
Outputs:
- grad_act: bfloat16 [16, 10240, 128], P('samples', ('groups', 'atoms')), parts along dimension 1
- grad_pair: bfloat16 [320, 32, 16, 128], P(('groups', 'atoms'), 'samples'), parts along dimension 0
- grad_weights: float32 [10, 128, 128], P('groups'), parts along dimension 0
- grad_pair_weight: float32 [32, 4], P('groups'), parts along dimension 0
- grad_token_weight: float32 [8], P('groups'), parts along dimension 0
The draws below stay inside these ranges and needn't reach their ends.
There are 2 independent parts, one for each index of `groups`. The reference program is written for one: setup_inputs(seed, part) draws one part's arguments, and reference() takes and returns one part's arrays. A program takes and returns all parts, laid end to end along the dimension named above; an argument that names none is the same for every part. Nothing has to cross between parts.
Inputs may be any that keep to these rules, and one draw needn't show every extreme that they name: Window w reads the 128 atoms that begin at 32 * w + offsets[w], moved into the complex. padding[r] atoms at the end of atom range r are padding. `atom_token`: the atoms of one token are contiguous, at most 24 of them.
All inputs are finite; a program needn't handle non-finite values.
Results may differ from the reference program's by a relative error of at most 0.025.
Values may be sent and summed in bfloat16 or wider, within the bound.
A program may use at most 128 MiB of HBM per device.

```python
import math
import jax
import jax.numpy as jnp
import numpy as np
from jax import lax

C = 128
HEADS = 4
CP = 16
WQ = 32
WK = 128
ATOM_DEV = 640
NATOMS = 5120
SAMPLES = 16
NWIN = 160
NTOK = 640
RANGES = 8
PAD_MOST = 64


def draw_pair(key, part):
    full_shape = (NWIN, WQ, CP, WK)
    key_one = jax.random.fold_in(key, 0)
    return jnp.clip(jax.random.normal(key_one, full_shape, jnp.float32), -6.0, 6.0).astype(jnp.bfloat16)


def draw_offsets(key, part):
    values = jax.random.randint(key, (NWIN,), -WK, WQ + 1, dtype=jnp.int32)
    middle = NWIN // 2
    return values.at[middle].set(-WK).at[middle + 1].set(WQ)


def draw_padding(key, part):
    values = jax.random.randint(key, (RANGES,), 0, PAD_MOST + 1, dtype=jnp.int32)
    return values.at[0].set(PAD_MOST).at[RANGES - 1].set(0)


def level_of(key, shape, shards, low, high):
    def one(axis_at, shards_of):
        heights = jax.random.uniform(jax.random.fold_in(jax.random.fold_in(key, 6), axis_at), (shards_of,), jnp.float32, low / len(shards), high / len(shards))
        return jnp.repeat(jnp.exp(heights), shape[axis_at] // shards_of).reshape((-1,) + (1,) * (len(shape) - axis_at - 1))

    level = one(*shards[0])
    for cut in shards[1:]:
        level = level * one(*cut)
    return level


def profile(number_of, total, limit, slope):
    portions = [(1 << 20) // math.isqrt(rank ** slope) + 1 for rank in range(2, number_of + 1)]
    surplus, counts = total - limit - (number_of - 1), [1] * (number_of - 1)
    while surplus > 0:
        movable = [i for i in range(number_of - 1) if counts[i] < limit]
        whole, remaining = sum([portions[i] for i in movable]), surplus
        for i in movable:
            addition = min(limit - counts[i], max(1, remaining * portions[i] // whole), surplus)
            counts[i] = counts[i] + addition
            surplus = surplus - addition
    return np.array([limit] + counts)


def uneven(key, number_of, total, most, skew):
    if number_of == 2:
        one = jax.random.randint(key, (), max(1, total - most), min(most, total - 1) + 1)
        return jnp.stack([one, total - one])
    tallies = jnp.asarray(profile(number_of, total, most, skew), jnp.int32)
    pairs = (number_of - 1) // 2
    donor, receiver = tallies[1:1 + 2 * pairs:2], tallies[2:2 + 2 * pairs:2]
    slack = jnp.minimum(donor - 1, most - receiver)
    passed = jax.random.randint(jax.random.fold_in(key, 1), (pairs,), 0, 1 << 20) % (slack + 1)
    tallies = tallies.at[1:1 + 2 * pairs:2].set(donor - passed).at[2:2 + 2 * pairs:2].set(receiver + passed)
    return tallies[jax.random.permutation(jax.random.fold_in(key, 2), number_of)]


def normal_values(key, extent, scale, limit, cuts=(), kind=jnp.bfloat16):
    result = jax.random.normal(key, extent, jnp.float32) * scale
    if len(cuts) > 0:
        result = level_of(key, extent, cuts, -0.22, 0.18) * result
    return jnp.clip(result, min=-limit, max=limit).astype(kind)


def setup_inputs(seed: int = 0, part: int = 0) -> dict:
    arg_keys = jax.random.split(jax.random.key(seed), 14)
    part_keys = jax.random.split(jax.random.fold_in(arg_keys[13], part), 14)
    act = normal_values(part_keys[0], (SAMPLES, NATOMS, C), 1.0, 6.0, ((0, 2), (1, 8)))
    grad_out = normal_values(part_keys[1], (SAMPLES, NATOMS, C), 1.0, 6.0, ((0, 2), (1, 8)))
    pair = draw_pair(jax.random.fold_in(jax.random.fold_in(arg_keys[13], part), 71), part)
    w_query = normal_values(arg_keys[3], (C, C), C ** -0.5, 0.5)
    w_key = normal_values(arg_keys[4], (C, C), C ** -0.5, 0.5)
    w_value = normal_values(arg_keys[5], (C, C), C ** -0.5, 0.5)
    w_gate = normal_values(arg_keys[6], (C, C), C ** -0.5, 0.5)
    w_out = normal_values(arg_keys[7], (C, C), C ** -0.5, 0.5)
    w_pair = normal_values(arg_keys[8], (CP, HEADS), CP ** -0.5, 1.5)
    w_token = jnp.clip(jax.random.uniform(arg_keys[9], (HEADS,), jnp.float32, -2.0, 2.0), -2.0, 2.0)
    offsets = draw_offsets(jax.random.fold_in(jax.random.fold_in(arg_keys[13], part), 71), part)
    atom_token = jnp.searchsorted(jnp.cumsum(uneven(part_keys[11], NTOK, NATOMS, 24, 2)), jnp.arange(NATOMS), side="right").astype(jnp.int32)
    padding = draw_padding(jax.random.fold_in(jax.random.fold_in(arg_keys[13], part), 71), part)
    return {"act": act, "grad_out": grad_out, "pair": pair, "w_query": w_query, "w_key": w_key, "w_value": w_value, "w_gate": w_gate, "w_out": w_out, "w_pair": w_pair, "w_token": w_token, "offsets": offsets, "atom_token": atom_token, "padding": padding}


MASKED = -1000000000.0

def float_einsum(pattern, left_op, right_op):
    return jnp.einsum(pattern, left_op.astype(jnp.float32), right_op.astype(jnp.float32), precision=lax.Precision.HIGHEST)

def window_layout(offsets, atom_token, padding):
    position = jnp.arange(NATOMS, dtype=jnp.int32)
    ranges = (position // ATOM_DEV).astype(jnp.int32)
    is_live = position % ATOM_DEV < ATOM_DEV - padding[ranges]
    starts = jnp.clip(WQ * jnp.arange(NWIN, dtype=jnp.int32) + offsets, 0, NATOMS - WK).astype(jnp.int32)
    key_rows = (starts[:, None] + jnp.arange(WK, dtype=jnp.int32)[None, :]).astype(jnp.int32)
    key_live = is_live[key_rows]
    same_token = atom_token.reshape(NWIN, WQ)[:, :, None] == atom_token[key_rows][:, None, :]
    return (key_rows, key_live, same_token)

def attend(query, keys, values, gate_logit, grad_y, pair_bias, key_live):
    windows = keys.shape[0]
    head_count = pair_bias.shape[1]
    channels = query.shape[-1]
    head_dim = channels // head_count
    score_scale = 1.0 / math.sqrt(head_dim)
    query_heads = query.reshape(windows, -1, head_count, head_dim)
    key_heads = keys.reshape(windows, -1, head_count, head_dim)
    value_heads = values.reshape(windows, -1, head_count, head_dim)
    scores = float_einsum('wihd,wjhd->whij', query_heads, key_heads) * score_scale + pair_bias
    scores = jnp.where(key_live[:, None, None, :], scores, MASKED)
    row_max = lax.optimization_barrier(jnp.max(scores, axis=-1, keepdims=True))
    exponent = jnp.exp(scores - row_max)
    attn_probs = exponent / lax.optimization_barrier(jnp.sum(exponent, axis=-1, keepdims=True))
    probs_b = attn_probs.astype(jnp.bfloat16)
    attended = float_einsum('whij,wjhd->wihd', probs_b, value_heads).reshape(query.shape)
    gate_value = jax.nn.sigmoid(gate_logit)
    gated = (gate_value * attended).astype(jnp.bfloat16)
    d_attended = (grad_y * gate_value).astype(jnp.bfloat16)
    d_gate = (grad_y * attended * gate_value * (1.0 - gate_value)).astype(jnp.bfloat16)
    attended_heads = d_attended.reshape(windows, -1, head_count, head_dim)
    d_probs = float_einsum('wihd,wjhd->whij', attended_heads, value_heads)
    d_scores = attn_probs * (d_probs - lax.optimization_barrier(jnp.sum(attn_probs * d_probs, axis=-1, keepdims=True)))
    ds_b = d_scores.astype(jnp.bfloat16)
    d_query = (float_einsum('whij,wjhd->wihd', ds_b, key_heads) * score_scale).astype(jnp.bfloat16).reshape(query.shape)
    d_keys = float_einsum('whij,wihd->wjhd', ds_b, query_heads) * score_scale
    d_values = float_einsum('whij,wihd->wjhd', probs_b, attended_heads)
    return (gated, d_query, d_gate, d_keys, d_values, d_scores)

def reference(act, grad_out, pair, w_query, w_key, w_value, w_gate, w_out, w_pair, w_token, offsets, atom_token, padding):
    key_rows, key_live, same_token = window_layout(offsets, atom_token, padding)
    same_float = same_token.astype(jnp.float32)
    pair_bias = float_einsum('wicj,ch->whij', pair, w_pair) + w_token[None, :, None, None] * same_float[:, None, :, :]
    projection = jnp.concatenate([w_query, w_key, w_value, w_gate], axis=1)

    def one_sample(running, inputs):
        bias_sum, weight_sum, out_sum = running
        sample_act, sample_grad = inputs
        mixed = jnp.dot(sample_act, projection, preferred_element_type=jnp.float32)
        query = mixed[:, :C].astype(jnp.bfloat16)
        keys = mixed[:, C:2 * C].astype(jnp.bfloat16)
        values = mixed[:, 2 * C:3 * C].astype(jnp.bfloat16)
        gate_logit = mixed[:, 3 * C:]
        grad_y = jnp.dot(sample_grad, w_out.T, preferred_element_type=jnp.float32)
        gated, d_query, d_gate, d_keys, d_values, d_scores = attend(query, keys[key_rows], values[key_rows], gate_logit, grad_y, pair_bias, key_live)
        key_grad = jnp.zeros((NATOMS, C), jnp.float32).at[key_rows].add(d_keys.reshape(NWIN, WK, C))
        value_grad = jnp.zeros((NATOMS, C), jnp.float32).at[key_rows].add(d_values.reshape(NWIN, WK, C))
        stacked = jnp.concatenate([d_query, key_grad.astype(jnp.bfloat16), value_grad.astype(jnp.bfloat16), d_gate], axis=1)
        grad_act = jnp.dot(stacked, projection.T, preferred_element_type=jnp.float32).astype(jnp.bfloat16)
        weight_sum = weight_sum + jnp.dot(sample_act.T, stacked, preferred_element_type=jnp.float32)
        out_sum = out_sum + jnp.dot(gated.T, sample_grad, preferred_element_type=jnp.float32)
        return ((bias_sum + d_scores, weight_sum, out_sum), grad_act)
    start_state = (jnp.zeros((NWIN, HEADS, WQ, WK), jnp.float32), jnp.zeros((C, 4 * C), jnp.float32), jnp.zeros((C, C), jnp.float32))
    (bias_total, weight_sum, out_sum), grad_act = lax.scan(one_sample, start_state, (act, grad_out))
    grad_pair = float_einsum('whij,ch->wicj', bias_total, w_pair).astype(jnp.bfloat16)
    grad_weights = jnp.concatenate([weight_sum.reshape(C, 4, C).transpose(1, 0, 2), out_sum[None]], axis=0)
    grad_pair_weight = float_einsum('wicj,whij->ch', pair, bias_total)
    grad_token_weight = lax.optimization_barrier(jnp.sum(bias_total * same_float[:, None, :, :], axis=(0, 2, 3)))
    return (grad_act, grad_pair, grad_weights, grad_pair_weight, grad_token_weight)
```

```python
import math

import jax
import jax.numpy as jnp
from jax import lax
from jax.experimental import pallas as pl
from jax.experimental.pallas import tpu as pltpu
from jax.sharding import PartitionSpec as P

MASKED = -1000000000.0
BF16 = jnp.bfloat16
F32 = jnp.float32


def nn(a, b):
    return lax.dot_general(a, b, (((1,), (0,)), ((), ())), preferred_element_type=F32)


def nt(a, b):
    return lax.dot_general(a, b, (((1,), (1,)), ((), ())), preferred_element_type=F32)


def tn(a, b):
    return lax.dot_general(a, b, (((0,), (0,)), ((), ())), preferred_element_type=F32)


def attention_kernel(
    heads,
    together,
    starts_ref,
    half_ref,
    act_ref,
    before_ref,
    after_ref,
    grad_ref,
    pair_ref,
    w_ref,
    wpair_ref,
    wtoken_ref,
    key_code_ref,
    query_code_ref,
    ga_ref,
    to_lower_ref,
    to_upper_ref,
    mine_ref,
    theirs_ref,
    sums_ref,
    wide_act,
    k_scr,
    v_scr,
    dk_scr,
    dv_scr,
    q_scr,
    gate_scr,
    gy_scr,
    dq_scr,
    dg_scr,
    gated_scr,
    pw_scr,
    tok_scr,
    bias_scr,
    ds_scr,
):
    samples, atoms, channels = act_ref.shape
    windows = pair_ref.shape[0]
    rows = atoms // windows
    halo = before_ref.shape[1]
    wide = atoms + 2 * halo
    span = halo
    head_dim = channels // heads
    scale = 1.0 / math.sqrt(head_dim)
    stack = heads * rows

    def project(s, carry):
        wide_act[s, 0:halo, :] = before_ref[s]
        wide_act[s, halo : halo + atoms, :] = act_ref[s]
        wide_act[s, halo + atoms : wide, :] = after_ref[s]
        full = wide_act[s]
        k_scr[s] = nn(full, w_ref[1]).astype(BF16).astype(F32)
        v_scr[s] = nn(full, w_ref[2]).astype(BF16).astype(F32)
        own = act_ref[s]
        q_scr[s] = nn(own, w_ref[0]).astype(BF16)
        gate_scr[s] = jax.nn.sigmoid(nn(own, w_ref[3]))
        gy_scr[s] = nt(grad_ref[s], w_ref[4])
        dk_scr[s] = jnp.zeros((wide, channels), F32)
        dv_scr[s] = jnp.zeros((wide, channels), F32)
        return carry

    lax.fori_loop(0, samples, project, 0)
    pw_scr[...] = jnp.zeros_like(pw_scr)
    tok_scr[...] = jnp.zeros_like(tok_scr)

    lane = lax.broadcasted_iota(jnp.int32, (rows, channels), 1) // head_dim
    head_is = [lane == h for h in range(heads)]

    def spread(x):
        wide_x = x.astype(F32)
        return jnp.concatenate(
            [jnp.where(head_is[h], wide_x, 0.0).astype(BF16) for h in range(heads)], axis=0
        )

    def collect(x):
        out = x[0:rows]
        for h in range(1, heads):
            out = jnp.where(head_is[h], x[h * rows : (h + 1) * rows], out)
        return out

    def window(w, carry):
        start = starts_ref[w]
        mine_rows = pl.ds(pl.multiple_of(w * rows, rows), rows)
        key_rows = pl.ds(start, span)
        key_code = key_code_ref[key_rows, :]
        same = key_code == query_code_ref[w]
        bias = tn(pair_ref[w], wpair_ref[...]) + jnp.where(same, wtoken_ref[...], 0.0)
        bias_scr[...] = jnp.where(key_code > 0.0, bias, MASKED)
        ds_scr[...] = jnp.zeros_like(ds_scr)

        def group(g, inner):
            ids = [g * together + u for u in range(together)]
            keys = [k_scr[s, key_rows, :].astype(BF16) for s in ids]
            values = [v_scr[s, key_rows, :].astype(BF16) for s in ids]
            qm = [spread(q_scr[s, mine_rows, :]) for s in ids]
            scores = [nt(k, q) * scale + bias_scr[...] for k, q in zip(keys, qm)]
            tops = [jnp.max(x, axis=0, keepdims=True) for x in scores]
            exps = [jnp.exp(x - t) for x, t in zip(scores, tops)]
            probs = [e * (1.0 / jnp.sum(e, axis=0, keepdims=True)) for e in exps]
            probs_b = [p.astype(BF16) for p in probs]
            attended = [collect(tn(p, v)) for p, v in zip(probs_b, values)]
            dam = []
            for s, a in zip(ids, attended):
                gate = gate_scr[s, mine_rows, :]
                gy = gy_scr[s, mine_rows, :]
                gated_scr[s, mine_rows, :] = (gate * a).astype(BF16)
                dg_scr[s, mine_rows, :] = (gy * a * gate * (1.0 - gate)).astype(BF16)
                dam.append(spread((gy * gate).astype(BF16)))
            dprobs = [nt(v, d) for v, d in zip(values, dam)]
            ds = [
                p * (d - jnp.sum(p * d, axis=0, keepdims=True)) for p, d in zip(probs, dprobs)
            ]
            ds_b = [d.astype(BF16) for d in ds]
            total = ds[0]
            for d in ds[1:]:
                total = total + d
            ds_scr[...] += total
            for i, s in enumerate(ids):
                dq_scr[s, mine_rows, :] = (collect(tn(ds_b[i], keys[i])) * scale).astype(BF16)
            for i, s in enumerate(ids):
                dk_scr[s, key_rows, :] += nn(ds_b[i], qm[i])
                dv_scr[s, key_rows, :] += nn(probs_b[i], dam[i])
            return inner

        lax.fori_loop(0, samples // together, group, 0)
        total = ds_scr[...]
        tok_scr[...] += jnp.where(same, total, 0.0)
        pw_scr[...] += nn(pair_ref[w], total.astype(BF16))
        turned = total.T
        half = rows // 2
        first_mine = half_ref[0] == 0
        for h in range(heads):
            low = turned[h * rows : h * rows + half]
            high = turned[h * rows + half : (h + 1) * rows]
            mine_ref[w, h * half : (h + 1) * half, :] = jnp.where(first_mine, low, high)
            theirs_ref[w, h * half : (h + 1) * half, :] = jnp.where(
                first_mine, high, low
            ).astype(BF16)
        return carry

    lax.fori_loop(0, windows, window, 0)

    sums_ref[...] = jnp.zeros_like(sums_ref)

    def finish(s, carry):
        dk = (dk_scr[s] * scale).astype(BF16)
        dv = dv_scr[s].astype(BF16)
        dq = dq_scr[s]
        dg = dg_scr[s]
        from_kv = nt(dk, w_ref[1]) + nt(dv, w_ref[2])
        to_lower_ref[s] = from_kv[0:halo].astype(BF16)
        to_upper_ref[s] = from_kv[halo + atoms : wide].astype(BF16)
        ga_ref[s] = from_kv[halo : halo + atoms] + nt(dq, w_ref[0]) + nt(dg, w_ref[3])
        own = act_ref[s]
        full = wide_act[s]
        c = channels
        sums_ref[0:c, :] += tn(own, dq)
        sums_ref[c : 2 * c, :] += tn(full, dk)
        sums_ref[2 * c : 3 * c, :] += tn(full, dv)
        sums_ref[3 * c : 4 * c, :] += tn(own, dg)
        sums_ref[4 * c : 5 * c, :] += tn(gated_scr[s], grad_ref[s])
        return carry

    lax.fori_loop(0, samples, finish, 0)
    pair_channels = pw_scr.shape[0] // rows
    shape = pw_scr.shape
    at_row = lax.broadcasted_iota(jnp.int32, shape, 0) // pair_channels
    at_col = lax.broadcasted_iota(jnp.int32, shape, 1) % rows
    diagonal = jnp.where(at_row == at_col, pw_scr[...], 0.0)
    base = 5 * channels
    sums_ref[base : base + pair_channels, :] = jnp.sum(
        diagonal.reshape(rows, pair_channels, stack), axis=0
    )
    sums_ref[base + pair_channels : base + pair_channels + 1, :] = jnp.sum(
        tok_scr[...], axis=0, keepdims=True
    )


def pair_kernel(mine_ref, got_ref, wt_ref, out_ref):
    def one(w, carry):
        total = mine_ref[w] + got_ref[w].astype(F32)
        high = total.astype(BF16)
        low = (total - high.astype(F32)).astype(BF16)
        weight = wt_ref[...]
        out_ref[w] = (nn(weight, high) + nn(weight, low)).astype(BF16)
        return carry

    lax.fori_loop(0, mine_ref.shape[0], one, 0)


def per_device(
    act,
    grad_out,
    pair,
    w_query,
    w_key,
    w_value,
    w_gate,
    w_out,
    w_pair,
    w_token,
    offsets,
    atom_token,
    padding,
):
    samples, atoms, channels = act.shape
    windows = offsets.shape[0]
    rows = atoms // windows
    pair_channels, heads = w_pair.shape
    span = pair.shape[-1]
    stack = heads * rows
    half = rows // 2
    ranges = lax.axis_size("atoms")
    wide = atoms + 2 * span
    up = [(i, i + 1) for i in range(ranges - 1)]
    down = [(i + 1, i) for i in range(ranges - 1)]

    before = lax.ppermute(act[:, atoms - span :], "atoms", up)
    after = lax.ppermute(act[:, :span], "atoms", down)
    position = jnp.arange(atoms, dtype=jnp.int32)
    codes = jnp.where(position < atoms - padding[0], atom_token + 1, 0)
    code_before = lax.ppermute(codes[atoms - span :], "atoms", up)
    code_after = lax.ppermute(codes[:span], "atoms", down)
    wide_codes = jnp.concatenate([code_before, codes, code_after]).astype(F32)
    key_code = jnp.broadcast_to(wide_codes[:, None], (wide, stack))
    query_code = jnp.tile((atom_token + 1).astype(F32).reshape(windows, 1, rows), (1, 1, heads))
    anchor = lax.axis_index("atoms") * atoms
    starts = (
        jnp.clip(
            anchor + rows * jnp.arange(windows, dtype=jnp.int32) + offsets,
            0,
            ranges * atoms - span,
        )
        - anchor
        + span
    )
    me = lax.axis_index("samples").astype(jnp.int32)
    eye = jnp.eye(rows, dtype=BF16)
    wpair_big = (eye[:, None, None, :] * w_pair[None, :, :, None]).reshape(
        rows * pair_channels, stack
    )
    eye_half = jnp.eye(half, dtype=BF16)
    wpair_half = (eye_half[:, None, None, :] * w_pair[None, :, :, None]).reshape(
        half * pair_channels, heads * half
    )
    wtoken_row = jnp.repeat(w_token, rows)[None, :]
    weights = jnp.stack([w_query, w_key, w_value, w_gate, w_out])

    together = 4 if samples % 4 == 0 else 1
    vmem = pl.BlockSpec(memory_space=pltpu.VMEM)
    smem = pl.BlockSpec(memory_space=pltpu.SMEM)
    sum_rows = 5 * channels + pair_channels + 8

    def kernel(*refs):
        attention_kernel(heads, together, *refs)

    ga, to_lower, to_upper, mine, theirs, sums = pl.pallas_call(
        kernel,
        out_shape=(
            jax.ShapeDtypeStruct((samples, atoms, channels), F32),
            jax.ShapeDtypeStruct((samples, span, channels), BF16),
            jax.ShapeDtypeStruct((samples, span, channels), BF16),
            jax.ShapeDtypeStruct((windows, heads * half, span), F32),
            jax.ShapeDtypeStruct((windows, heads * half, span), BF16),
            jax.ShapeDtypeStruct((sum_rows, channels), F32),
        ),
        in_specs=[smem, smem] + [vmem] * 10,
        out_specs=(vmem,) * 6,
        scratch_shapes=[
            pltpu.VMEM((samples, wide, channels), BF16),
            pltpu.VMEM((samples, wide, channels), F32),
            pltpu.VMEM((samples, wide, channels), F32),
            pltpu.VMEM((samples, wide, channels), F32),
            pltpu.VMEM((samples, wide, channels), F32),
            pltpu.VMEM((samples, atoms, channels), BF16),
            pltpu.VMEM((samples, atoms, channels), F32),
            pltpu.VMEM((samples, atoms, channels), F32),
            pltpu.VMEM((samples, atoms, channels), BF16),
            pltpu.VMEM((samples, atoms, channels), BF16),
            pltpu.VMEM((samples, atoms, channels), BF16),
            pltpu.VMEM((rows * pair_channels, stack), F32),
            pltpu.VMEM((span, stack), F32),
            pltpu.VMEM((span, stack), F32),
            pltpu.VMEM((span, stack), F32),
        ],
        compiler_params=pltpu.CompilerParams(vmem_limit_bytes=56 * 1024 * 1024),
        name="attention",
    )(
        starts,
        me.reshape(1),
        act,
        before,
        after,
        grad_out,
        pair.reshape(windows, rows * pair_channels, span),
        weights,
        wpair_big,
        wtoken_row,
        key_code,
        query_code,
    )

    from_upper = lax.ppermute(to_lower, "atoms", down).astype(F32)
    from_lower = lax.ppermute(to_upper, "atoms", up).astype(F32)
    count = lax.axis_size("samples")
    got = lax.ppermute(theirs, "samples", [(i, (i + 1) % count) for i in range(count)])
    total = lax.psum(sums, ("atoms", "samples"))

    grad_act = jnp.concatenate(
        [
            ga[:, :span] + from_lower,
            ga[:, span : atoms - span],
            ga[:, atoms - span :] + from_upper,
        ],
        axis=1,
    ).astype(BF16)
    grad_pair = pl.pallas_call(
        pair_kernel,
        out_shape=jax.ShapeDtypeStruct((windows, half * pair_channels, span), BF16),
        in_specs=[vmem] * 3,
        out_specs=vmem,
        name="pair_grad",
    )(mine, got, wpair_half).reshape(windows, half, pair_channels, span)

    base = 5 * channels
    grad_weights = total[:base].reshape(5, channels, channels)
    grad_pair_weight = jnp.sum(
        total[base : base + pair_channels].reshape(pair_channels, heads, rows), axis=-1
    )
    grad_token_weight = jnp.sum(total[base + pair_channels].reshape(heads, rows), axis=-1)
    return (grad_act, grad_pair, grad_weights, grad_pair_weight, grad_token_weight)


def solution(mesh):
    in_specs = (
        P("samples", ("groups", "atoms"), None),
        P("samples", ("groups", "atoms"), None),
        P(("groups", "atoms"), None, None, None),
        P(),
        P(),
        P(),
        P(),
        P(),
        P(),
        P(),
        P(("groups", "atoms")),
        P(("groups", "atoms")),
        P(("groups", "atoms")),
    )
    out_specs = (
        P("samples", ("groups", "atoms"), None),
        P(("groups", "atoms"), "samples", None, None),
        P("groups", None, None),
        P("groups", None),
        P("groups"),
    )
    return jax.shard_map(
        per_device, mesh=mesh, in_specs=in_specs, out_specs=out_specs, check_vma=False
    )
```

```python
import math

import jax
import jax.numpy as jnp
from jax import lax
from jax.experimental import pallas as pl
from jax.experimental.pallas import tpu as pltpu
from jax.sharding import PartitionSpec as P

MASKED = -1000000000.0
BF16 = jnp.bfloat16
F32 = jnp.float32


def nn(a, b):
    return lax.dot_general(a, b, (((1,), (0,)), ((), ())), preferred_element_type=F32)


def nt(a, b):
    return lax.dot_general(a, b, (((1,), (1,)), ((), ())), preferred_element_type=F32)


def tn(a, b):
    return lax.dot_general(a, b, (((0,), (0,)), ((), ())), preferred_element_type=F32)


def attention_kernel(
    heads,
    together,
    offsets_ref,
    wtoken_ref,
    act_ref,
    before_ref,
    after_ref,
    grad_ref,
    pair_ref,
    wq_ref,
    wk_ref,
    wv_ref,
    wg_ref,
    wo_ref,
    wpair_ref,
    code_ref,
    code_before_ref,
    code_after_ref,
    query_code_ref,
    ga_ref,
    to_lower_ref,
    to_upper_ref,
    mine_ref,
    theirs_ref,
    sums_ref,
    wide_act,
    k_scr,
    v_scr,
    dk_scr,
    dv_scr,
    q_scr,
    gate_scr,
    gy_scr,
    dq_scr,
    dg_scr,
    gated_scr,
    pw_scr,
    tok_scr,
    bias_scr,
    ds_scr,
    key_code_scr,
    wpair_scr,
):
    samples, atoms, channels = act_ref.shape
    windows = pair_ref.shape[0]
    rows = atoms // windows
    halo = before_ref.shape[1]
    wide = atoms + 2 * halo
    span = halo
    head_dim = channels // heads
    scale = 1.0 / math.sqrt(head_dim)
    stack = heads * rows

    def project(s, carry):
        wide_act[s, 0:halo, :] = before_ref[s]
        wide_act[s, halo : halo + atoms, :] = act_ref[s]
        wide_act[s, halo + atoms : wide, :] = after_ref[s]
        full = wide_act[s]
        k_scr[s] = nn(full, wk_ref[...]).astype(BF16).astype(F32)
        v_scr[s] = nn(full, wv_ref[...]).astype(BF16).astype(F32)
        own = act_ref[s]
        q_scr[s] = nn(own, wq_ref[...]).astype(BF16)
        gate_scr[s] = jax.nn.sigmoid(nn(own, wg_ref[...]))
        gy_scr[s] = nt(grad_ref[s], wo_ref[...])
        dk_scr[s] = jnp.zeros((wide, channels), F32)
        dv_scr[s] = jnp.zeros((wide, channels), F32)
        return carry

    lax.fori_loop(0, samples, project, 0)
    pw_scr[...] = jnp.zeros_like(pw_scr)
    tok_scr[...] = jnp.zeros_like(tok_scr)

    def code_column(first, row):
        column = jnp.broadcast_to(row.astype(F32), (stack, span)).T
        key_code_scr[first : first + span, :] = column

    code_column(0, code_before_ref[0])
    for r in range(atoms // span):
        code_column(halo + r * span, code_ref[r])
    code_column(halo + atoms, code_after_ref[0])

    pair_channels = wpair_ref.shape[0]
    lane_head = lax.broadcasted_iota(jnp.int32, (pair_channels, stack), 1) // rows
    wpair_values = wpair_ref[...].astype(F32)
    wpair_rows = jnp.zeros((pair_channels, stack), F32)
    wtoken_row = jnp.zeros((1, stack), F32)
    for h in range(heads):
        wpair_rows = jnp.where(lane_head == h, wpair_values[:, h : h + 1], wpair_rows)
        wtoken_row = jnp.where(lane_head[0:1] == h, wtoken_ref[h], wtoken_row)
    lane_row = lax.broadcasted_iota(jnp.int32, (pair_channels, stack), 1) % rows
    for i in range(rows):
        wpair_scr[i * pair_channels : (i + 1) * pair_channels, :] = jnp.where(
            lane_row == i, wpair_rows, 0.0
        ).astype(BF16)
    anchor = lax.axis_index("atoms") * atoms
    last_start = lax.axis_size("atoms") * atoms - span
    first_mine = lax.axis_index("samples") == 0

    lane = lax.broadcasted_iota(jnp.int32, (rows, channels), 1) // head_dim
    head_is = [lane == h for h in range(heads)]

    def spread(x):
        wide_x = x.astype(F32)
        return jnp.concatenate(
            [jnp.where(head_is[h], wide_x, 0.0).astype(BF16) for h in range(heads)], axis=0
        )

    def collect(x):
        out = x[0:rows]
        for h in range(1, heads):
            out = jnp.where(head_is[h], x[h * rows : (h + 1) * rows], out)
        return out

    def window(w, carry):
        start = jnp.clip(anchor + w * rows + offsets_ref[w], 0, last_start) - anchor + span
        mine_rows = pl.ds(pl.multiple_of(w * rows, rows), rows)
        key_rows = pl.ds(start, span)
        key_code = key_code_scr[key_rows, :]
        same = key_code == query_code_ref[w].astype(F32)
        bias = tn(pair_ref[w], wpair_scr[...]) + jnp.where(same, wtoken_row, 0.0)
        bias_scr[...] = jnp.where(key_code > 0.0, bias, MASKED)
        ds_scr[...] = jnp.zeros_like(ds_scr)

        def group(g, inner):
            ids = [g * together + u for u in range(together)]
            keys = [k_scr[s, key_rows, :].astype(BF16) for s in ids]
            values = [v_scr[s, key_rows, :].astype(BF16) for s in ids]
            qm = [spread(q_scr[s, mine_rows, :]) for s in ids]
            scores = [nt(k, q) * scale + bias_scr[...] for k, q in zip(keys, qm)]
            tops = [jnp.max(x, axis=0, keepdims=True) for x in scores]
            exps = [jnp.exp(x - t) for x, t in zip(scores, tops)]
            probs = [e * (1.0 / jnp.sum(e, axis=0, keepdims=True)) for e in exps]
            probs_b = [p.astype(BF16) for p in probs]
            attended = [collect(tn(p, v)) for p, v in zip(probs_b, values)]
            dam = []
            for s, a in zip(ids, attended):
                gate = gate_scr[s, mine_rows, :]
                gy = gy_scr[s, mine_rows, :]
                gated_scr[s, mine_rows, :] = (gate * a).astype(BF16)
                dg_scr[s, mine_rows, :] = (gy * a * gate * (1.0 - gate)).astype(BF16)
                dam.append(spread((gy * gate).astype(BF16)))
            dprobs = [nt(v, d) for v, d in zip(values, dam)]
            ds = [
                p * (d - jnp.sum(p * d, axis=0, keepdims=True)) for p, d in zip(probs, dprobs)
            ]
            ds_b = [d.astype(BF16) for d in ds]
            total = ds[0]
            for d in ds[1:]:
                total = total + d
            ds_scr[...] += total
            for i, s in enumerate(ids):
                dq_scr[s, mine_rows, :] = (collect(tn(ds_b[i], keys[i])) * scale).astype(BF16)
            for i, s in enumerate(ids):
                dk_scr[s, key_rows, :] += nn(ds_b[i], qm[i])
                dv_scr[s, key_rows, :] += nn(probs_b[i], dam[i])
            return inner

        lax.fori_loop(0, samples // together, group, 0)
        total = ds_scr[...]
        tok_scr[...] += jnp.where(same, total, 0.0)
        pw_scr[...] += nn(pair_ref[w], total.astype(BF16))
        turned = total.T
        half = rows // 2
        for h in range(heads):
            low = turned[h * rows : h * rows + half]
            high = turned[h * rows + half : (h + 1) * rows]
            mine_ref[w, h * half : (h + 1) * half, :] = jnp.where(first_mine, low, high)
            theirs_ref[w, h * half : (h + 1) * half, :] = jnp.where(
                first_mine, high, low
            ).astype(BF16)
        return carry

    lax.fori_loop(0, windows, window, 0)

    sums_ref[...] = jnp.zeros_like(sums_ref)

    def finish(s, carry):
        dk = (dk_scr[s] * scale).astype(BF16)
        dv = dv_scr[s].astype(BF16)
        dq = dq_scr[s]
        dg = dg_scr[s]
        from_kv = nt(dk, wk_ref[...]) + nt(dv, wv_ref[...])
        to_lower_ref[s] = from_kv[0:halo].astype(BF16)
        to_upper_ref[s] = from_kv[halo + atoms : wide].astype(BF16)
        ga_ref[s] = from_kv[halo : halo + atoms] + nt(dq, wq_ref[...]) + nt(dg, wg_ref[...])
        own = act_ref[s]
        full = wide_act[s]
        c = channels
        sums_ref[0:c, :] += tn(own, dq)
        sums_ref[c : 2 * c, :] += tn(full, dk)
        sums_ref[2 * c : 3 * c, :] += tn(full, dv)
        sums_ref[3 * c : 4 * c, :] += tn(own, dg)
        sums_ref[4 * c : 5 * c, :] += tn(gated_scr[s], grad_ref[s])
        return carry

    lax.fori_loop(0, samples, finish, 0)
    shape = pw_scr.shape
    at_row = lax.broadcasted_iota(jnp.int32, shape, 0) // pair_channels
    at_col = lax.broadcasted_iota(jnp.int32, shape, 1) % rows
    diagonal = jnp.where(at_row == at_col, pw_scr[...], 0.0)
    base = 5 * channels
    sums_ref[base : base + pair_channels, :] = jnp.sum(
        diagonal.reshape(rows, pair_channels, stack), axis=0
    )
    sums_ref[base + pair_channels : base + pair_channels + 1, :] = jnp.sum(
        tok_scr[...], axis=0, keepdims=True
    )


def greet(barrier, devices):
    for device in devices:
        pl.semaphore_signal(
            barrier, inc=1, device_id=device, device_id_type=pl.DeviceIdType.MESH
        )


def remote(src, dst, sems, slot, device):
    return pltpu.make_async_remote_copy(
        src_ref=src,
        dst_ref=dst,
        send_sem=sems.at[0, slot],
        recv_sem=sems.at[1, slot],
        device_id=device,
        device_id_type=pl.DeviceIdType.MESH,
    )


def halo_kernel(
    ranges,
    span,
    act_ref,
    code_ref,
    before_ref,
    after_ref,
    code_before_ref,
    code_after_ref,
    sems,
):
    me = lax.axis_index("atoms")
    atoms = act_ref.shape[1]
    has_lower, has_upper = me > 0, me < ranges - 1
    lower, upper = {"atoms": me - 1}, {"atoms": me + 1}
    barrier = pltpu.get_barrier_semaphore()

    @pl.when(has_lower)
    def _():
        greet(barrier, [lower])

    @pl.when(has_upper)
    def _():
        greet(barrier, [upper])

    inside = jnp.logical_and(has_lower, has_upper)

    @pl.when(inside)
    def _():
        pl.semaphore_wait(barrier, 2)

    @pl.when(jnp.logical_not(inside))
    def _():
        pl.semaphore_wait(barrier, 1)

    last = code_ref.shape[0] - 1
    to_upper = [
        remote(act_ref.at[:, pl.ds(atoms - span, span)], before_ref, sems, 0, upper),
        remote(code_ref.at[pl.ds(last, 1)], code_before_ref, sems, 1, upper),
    ]
    to_lower = [
        remote(act_ref.at[:, pl.ds(0, span)], after_ref, sems, 2, lower),
        remote(code_ref.at[pl.ds(0, 1)], code_after_ref, sems, 3, lower),
    ]

    @pl.when(has_upper)
    def _():
        for copy in to_upper:
            copy.start()

    @pl.when(has_lower)
    def _():
        for copy in to_lower:
            copy.start()

    @pl.when(jnp.logical_not(has_lower))
    def _():
        before_ref[...] = jnp.zeros_like(before_ref)
        code_before_ref[...] = jnp.zeros_like(code_before_ref)

    @pl.when(jnp.logical_not(has_upper))
    def _():
        after_ref[...] = jnp.zeros_like(after_ref)
        code_after_ref[...] = jnp.zeros_like(code_after_ref)

    @pl.when(has_upper)
    def _():
        for copy in to_upper:
            copy.wait_send()
        for copy in to_lower:
            copy.wait_recv()

    @pl.when(has_lower)
    def _():
        for copy in to_lower:
            copy.wait_send()
        for copy in to_upper:
            copy.wait_recv()


def exchange_kernel(
    ranges,
    ga_ref,
    to_lower_ref,
    to_upper_ref,
    mine_ref,
    theirs_ref,
    sums_ref,
    wpair_ref,
    out_ref,
    pair_out_ref,
    total_ref,
    from_lower,
    from_upper,
    got,
    got_half,
    part,
    slots,
    wpair_scr,
    edge_sems,
    core_sems,
    scatter_sems,
    gather_sems,
):
    me = lax.axis_index("atoms")
    core = lax.axis_index("samples")
    other = 1 - core
    samples, atoms, channels = ga_ref.shape
    span = to_lower_ref.shape[1]
    chunk = part.shape[1]
    half = ranges * chunk
    has_lower, has_upper = me > 0, me < ranges - 1
    lower, upper, peer = {"atoms": me - 1}, {"atoms": me + 1}, {"samples": other}
    everyone = [{"atoms": lax.rem(me + d, ranges)} for d in range(1, ranges)]
    barrier = pltpu.get_barrier_semaphore()
    greet(barrier, [peer] + everyone)
    pl.semaphore_wait(barrier, ranges)

    half_copy = remote(
        sums_ref.at[pl.ds(pl.multiple_of(other * half, 8), half)], got_half, core_sems, 0, peer
    )
    half_copy.start()
    pair_copy = remote(theirs_ref, got, core_sems, 1, peer)
    pair_copy.start()
    up_copy = remote(to_upper_ref, from_lower, edge_sems, 0, upper)
    down_copy = remote(to_lower_ref, from_upper, edge_sems, 1, lower)

    half_copy.wait_recv()
    own_half = pl.ds(pl.multiple_of(core * half, 8), half)
    part[...] = (sums_ref[own_half, :] + got_half[...]).reshape(part.shape)
    scatter = []
    for d in range(1, ranges):
        target = lax.rem(me + d, ranges)
        copy = remote(part.at[target], slots.at[d - 1], scatter_sems, d - 1, everyone[d - 1])
        copy.start()
        scatter.append(copy)

    @pl.when(has_upper)
    def _():
        up_copy.start()

    @pl.when(has_lower)
    def _():
        down_copy.start()

    pair_channels, heads = wpair_ref.shape
    rows = mine_ref.shape[1] // heads
    stack = heads * rows
    lane = lax.broadcasted_iota(jnp.int32, (pair_channels, stack), 1)
    values = wpair_ref[...].astype(F32)
    wpair_rows = jnp.zeros((pair_channels, stack), F32)
    for h in range(heads):
        wpair_rows = jnp.where(lane // rows == h, values[:, h : h + 1], wpair_rows)
    for i in range(rows):
        wpair_scr[i * pair_channels : (i + 1) * pair_channels, :] = jnp.where(
            lane % rows == i, wpair_rows, 0.0
        ).astype(BF16)

    for copy in scatter:
        copy.wait_recv()
    chunk_total = part[me]
    for d in range(1, ranges):
        chunk_total = chunk_total + slots[d - 1]
    place = pl.ds(pl.multiple_of(core * half + me * chunk, 8), chunk)
    total_ref[place, :] = chunk_total
    gather = []
    for d in range(1, ranges):
        copy = remote(
            total_ref.at[place], total_ref.at[place], gather_sems, d - 1, everyone[d - 1]
        )
        copy.start()
        gather.append(copy)

    pair_copy.wait_recv()

    def one_window(w, carry):
        both = mine_ref[w] + got[w].astype(F32)
        high = both.astype(BF16)
        low = (both - high.astype(F32)).astype(BF16)
        weight = wpair_scr[...]
        pair_out_ref[w] = (nn(weight, high) + nn(weight, low)).astype(BF16)
        return carry

    lax.fori_loop(0, mine_ref.shape[0], one_window, 0)

    for copy in gather:
        copy.wait_recv()
    last_copy = remote(
        total_ref.at[own_half], total_ref.at[own_half], core_sems, 2, peer
    )
    last_copy.start()

    @pl.when(has_lower)
    def _():
        down_copy.wait_send()
        up_copy.wait_recv()

    @pl.when(has_upper)
    def _():
        up_copy.wait_send()
        down_copy.wait_recv()

    @pl.when(jnp.logical_not(has_lower))
    def _():
        from_lower[...] = jnp.zeros_like(from_lower)

    @pl.when(jnp.logical_not(has_upper))
    def _():
        from_upper[...] = jnp.zeros_like(from_upper)

    def one_sample(s, carry):
        out_ref[s, 0:span, :] = (ga_ref[s, 0:span, :] + from_lower[s].astype(F32)).astype(BF16)
        out_ref[s, span : atoms - span, :] = ga_ref[s, span : atoms - span, :].astype(BF16)
        out_ref[s, atoms - span : atoms, :] = (
            ga_ref[s, atoms - span : atoms, :] + from_upper[s].astype(F32)
        ).astype(BF16)
        return carry

    lax.fori_loop(0, samples, one_sample, 0)
    half_copy.wait_send()
    pair_copy.wait_send()
    for copy in scatter + gather:
        copy.wait_send()
    last_copy.wait()


def per_device(
    act,
    grad_out,
    pair,
    w_query,
    w_key,
    w_value,
    w_gate,
    w_out,
    w_pair,
    w_token,
    offsets,
    atom_token,
    padding,
):
    samples, atoms, channels = act.shape
    windows = offsets.shape[0]
    rows = atoms // windows
    pair_channels, heads = w_pair.shape
    span = pair.shape[-1]
    stack = heads * rows
    half = rows // 2
    ranges = lax.axis_size("atoms")
    wide = atoms + 2 * span
    vmem = pl.BlockSpec(memory_space=pltpu.VMEM)
    smem = pl.BlockSpec(memory_space=pltpu.SMEM)
    position = jnp.arange(atoms, dtype=jnp.int32)
    codes = jnp.where(position < atoms - padding[0], atom_token + 1, 0)
    codes = codes.reshape(atoms // span, 1, span)
    query_code = jnp.tile((atom_token + 1).reshape(windows, 1, rows), (1, 1, heads))

    def first_kernel(*refs):
        halo_kernel(ranges, span, *refs)

    before, after, code_before, code_after = pl.pallas_call(
        first_kernel,
        out_shape=(
            jax.ShapeDtypeStruct((samples, span, channels), BF16),
            jax.ShapeDtypeStruct((samples, span, channels), BF16),
            jax.ShapeDtypeStruct((1, 1, span), jnp.int32),
            jax.ShapeDtypeStruct((1, 1, span), jnp.int32),
        ),
        in_specs=[pl.BlockSpec(memory_space=pl.ANY), vmem],
        out_specs=(vmem,) * 4,
        scratch_shapes=[pltpu.SemaphoreType.DMA((2, 4))],
        compiler_params=pltpu.CompilerParams(collective_id=0, has_side_effects=True),
        name="halo",
    )(act, codes)

    together = 4 if samples % 4 == 0 else 1
    chunk = 8 * pl.cdiv(5 * channels + pair_channels + 1, 16 * ranges)
    sum_rows = 2 * ranges * chunk

    def kernel(*refs):
        attention_kernel(heads, together, *refs)

    ga, to_lower, to_upper, mine, theirs, sums = pl.pallas_call(
        kernel,
        out_shape=(
            jax.ShapeDtypeStruct((samples, atoms, channels), F32),
            jax.ShapeDtypeStruct((samples, span, channels), BF16),
            jax.ShapeDtypeStruct((samples, span, channels), BF16),
            jax.ShapeDtypeStruct((windows, heads * half, span), F32),
            jax.ShapeDtypeStruct((windows, heads * half, span), BF16),
            jax.ShapeDtypeStruct((sum_rows, channels), F32),
        ),
        in_specs=[smem, smem] + [vmem] * 15,
        out_specs=(vmem,) * 6,
        scratch_shapes=[
            pltpu.VMEM((samples, wide, channels), BF16),
            pltpu.VMEM((samples, wide, channels), F32),
            pltpu.VMEM((samples, wide, channels), F32),
            pltpu.VMEM((samples, wide, channels), F32),
            pltpu.VMEM((samples, wide, channels), F32),
            pltpu.VMEM((samples, atoms, channels), BF16),
            pltpu.VMEM((samples, atoms, channels), F32),
            pltpu.VMEM((samples, atoms, channels), F32),
            pltpu.VMEM((samples, atoms, channels), BF16),
            pltpu.VMEM((samples, atoms, channels), BF16),
            pltpu.VMEM((samples, atoms, channels), BF16),
            pltpu.VMEM((rows * pair_channels, stack), F32),
            pltpu.VMEM((span, stack), F32),
            pltpu.VMEM((span, stack), F32),
            pltpu.VMEM((span, stack), F32),
            pltpu.VMEM((wide, stack), F32),
            pltpu.VMEM((rows * pair_channels, stack), BF16),
        ],
        compiler_params=pltpu.CompilerParams(vmem_limit_bytes=56 * 1024 * 1024),
        name="attention",
    )(
        offsets,
        w_token,
        act,
        before,
        after,
        grad_out,
        pair.reshape(windows, rows * pair_channels, span),
        w_query,
        w_key,
        w_value,
        w_gate,
        w_out,
        w_pair,
        codes,
        code_before,
        code_after,
        query_code,
    )

    def last_kernel(*refs):
        exchange_kernel(ranges, *refs)

    edge = pltpu.VMEM((samples, span, channels), BF16)
    grad_act, grad_pair, total = pl.pallas_call(
        last_kernel,
        out_shape=(
            jax.ShapeDtypeStruct((samples, atoms, channels), BF16),
            jax.ShapeDtypeStruct((windows, half * pair_channels, span), BF16),
            jax.ShapeDtypeStruct((sum_rows, channels), F32),
        ),
        in_specs=[vmem] * 7,
        out_specs=(vmem,) * 3,
        scratch_shapes=[
            edge,
            edge,
            pltpu.VMEM((windows, heads * half, span), BF16),
            pltpu.VMEM((ranges * chunk, channels), F32),
            pltpu.VMEM((ranges, chunk, channels), F32),
            pltpu.VMEM((ranges - 1, chunk, channels), F32),
            pltpu.VMEM((half * pair_channels, heads * half), BF16),
            pltpu.SemaphoreType.DMA((2, 2)),
            pltpu.SemaphoreType.DMA((2, 3)),
            pltpu.SemaphoreType.DMA((2, ranges - 1)),
            pltpu.SemaphoreType.DMA((2, ranges - 1)),
        ],
        compiler_params=pltpu.CompilerParams(
            collective_id=1, has_side_effects=True, vmem_limit_bytes=40 * 1024 * 1024
        ),
        name="exchange",
    )(ga, to_lower, to_upper, mine, theirs, sums, w_pair)

    base = 5 * channels
    grad_weights = total[:base].reshape(5, channels, channels)
    grad_pair_weight = jnp.sum(
        total[base : base + pair_channels].reshape(pair_channels, heads, rows), axis=-1
    )
    grad_token_weight = jnp.sum(total[base + pair_channels].reshape(heads, rows), axis=-1)
    grad_pair = grad_pair.reshape(windows, half, pair_channels, span)
    return (grad_act, grad_pair, grad_weights, grad_pair_weight, grad_token_weight)


def solution(mesh):
    in_specs = (
        P("samples", ("groups", "atoms"), None),
        P("samples", ("groups", "atoms"), None),
        P(("groups", "atoms"), None, None, None),
        P(),
        P(),
        P(),
        P(),
        P(),
        P(),
        P(),
        P(("groups", "atoms")),
        P(("groups", "atoms")),
        P(("groups", "atoms")),
    )
    out_specs = (
        P("samples", ("groups", "atoms"), None),
        P(("groups", "atoms"), "samples", None, None),
        P("groups", None, None),
        P("groups", None),
        P("groups"),
    )
    return jax.shard_map(
        per_device, mesh=mesh, in_specs=in_specs, out_specs=out_specs, check_vma=False
    )
```

```python
import math

import jax
import jax.numpy as jnp
from jax import lax
from jax.experimental import pallas as pl
from jax.experimental.pallas import tpu as pltpu
from jax.sharding import PartitionSpec as P

MASKED = -1000000000.0
BF16 = jnp.bfloat16
F32 = jnp.float32


def nn(a, b):
    return lax.dot_general(a, b, (((1,), (0,)), ((), ())), preferred_element_type=F32)


def nt(a, b):
    return lax.dot_general(a, b, (((1,), (1,)), ((), ())), preferred_element_type=F32)


def tn(a, b):
    return lax.dot_general(a, b, (((0,), (0,)), ((), ())), preferred_element_type=F32)


def attention_kernel(
    heads,
    together,
    offsets_ref,
    wtoken_ref,
    act_ref,
    before_ref,
    after_ref,
    grad_ref,
    pair_ref,
    wq_ref,
    wk_ref,
    wv_ref,
    wg_ref,
    wo_ref,
    wpair_ref,
    code_ref,
    code_before_ref,
    code_after_ref,
    query_code_ref,
    ga_ref,
    to_lower_ref,
    to_upper_ref,
    mine_ref,
    theirs_ref,
    sums_ref,
    wide_act,
    k_scr,
    v_scr,
    dk_scr,
    dv_scr,
    q_scr,
    gate_scr,
    gy_scr,
    dq_scr,
    dg_scr,
    gated_scr,
    pw_scr,
    tok_scr,
    bias_scr,
    ds_scr,
    key_code_scr,
    wpair_scr,
):
    samples, atoms, channels = act_ref.shape
    windows = pair_ref.shape[0]
    rows = atoms // windows
    halo = before_ref.shape[1]
    wide = atoms + 2 * halo
    span = halo
    head_dim = channels // heads
    scale = 1.0 / math.sqrt(head_dim)
    stack = heads * rows

    def project(s, carry):
        wide_act[s, 0:halo, :] = before_ref[s]
        wide_act[s, halo : halo + atoms, :] = act_ref[s]
        wide_act[s, halo + atoms : wide, :] = after_ref[s]
        full = wide_act[s]
        k_scr[s] = nn(full, wk_ref[...]).astype(BF16).astype(F32)
        v_scr[s] = nn(full, wv_ref[...]).astype(BF16).astype(F32)
        own = act_ref[s]
        q_scr[s] = nn(own, wq_ref[...]).astype(BF16)
        gate_scr[s] = jax.nn.sigmoid(nn(own, wg_ref[...]))
        gy_scr[s] = nt(grad_ref[s], wo_ref[...])
        dk_scr[s] = jnp.zeros((wide, channels), F32)
        dv_scr[s] = jnp.zeros((wide, channels), F32)
        return carry

    lax.fori_loop(0, samples, project, 0)
    pw_scr[...] = jnp.zeros_like(pw_scr)
    tok_scr[...] = jnp.zeros_like(tok_scr)

    def code_column(first, row):
        column = jnp.broadcast_to(row.astype(F32), (stack, span)).T
        key_code_scr[first : first + span, :] = column

    code_column(0, code_before_ref[0])
    for r in range(atoms // span):
        code_column(halo + r * span, code_ref[r])
    code_column(halo + atoms, code_after_ref[0])

    pair_channels = wpair_ref.shape[0]
    lane_head = lax.broadcasted_iota(jnp.int32, (pair_channels, stack), 1) // rows
    wpair_values = wpair_ref[...].astype(F32)
    wpair_rows = jnp.zeros((pair_channels, stack), F32)
    wtoken_row = jnp.zeros((1, stack), F32)
    for h in range(heads):
        wpair_rows = jnp.where(lane_head == h, wpair_values[:, h : h + 1], wpair_rows)
        wtoken_row = jnp.where(lane_head[0:1] == h, wtoken_ref[h], wtoken_row)
    lane_row = lax.broadcasted_iota(jnp.int32, (pair_channels, stack), 1) % rows
    for i in range(rows):
        wpair_scr[i * pair_channels : (i + 1) * pair_channels, :] = jnp.where(
            lane_row == i, wpair_rows, 0.0
        ).astype(BF16)
    anchor = lax.axis_index("atoms") * atoms
    last_start = lax.axis_size("atoms") * atoms - span
    first_mine = lax.axis_index("samples") == 0

    lane = lax.broadcasted_iota(jnp.int32, (rows, channels), 1) // head_dim
    head_is = [lane == h for h in range(heads)]

    def spread(x):
        wide_x = x.astype(F32)
        return jnp.concatenate(
            [jnp.where(head_is[h], wide_x, 0.0).astype(BF16) for h in range(heads)], axis=0
        )

    def collect(x):
        out = x[0:rows]
        for h in range(1, heads):
            out = jnp.where(head_is[h], x[h * rows : (h + 1) * rows], out)
        return out

    def window(w, carry):
        start = jnp.clip(anchor + w * rows + offsets_ref[w], 0, last_start) - anchor + span
        mine_rows = pl.ds(pl.multiple_of(w * rows, rows), rows)
        key_rows = pl.ds(start, span)
        key_code = key_code_scr[key_rows, :]
        same = key_code == query_code_ref[w].astype(F32)
        bias = tn(pair_ref[w], wpair_scr[...]) + jnp.where(same, wtoken_row, 0.0)
        bias_scr[...] = jnp.where(key_code > 0.0, bias, MASKED)
        ds_scr[...] = jnp.zeros_like(ds_scr)

        def group(g, inner):
            ids = [g * together + u for u in range(together)]
            keys = [k_scr[s, key_rows, :].astype(BF16) for s in ids]
            values = [v_scr[s, key_rows, :].astype(BF16) for s in ids]
            qm = [spread(q_scr[s, mine_rows, :]) for s in ids]
            scores = [nt(k, q) * scale + bias_scr[...] for k, q in zip(keys, qm)]
            tops = [jnp.max(x, axis=0, keepdims=True) for x in scores]
            exps = [jnp.exp(x - t) for x, t in zip(scores, tops)]
            probs = [e * (1.0 / jnp.sum(e, axis=0, keepdims=True)) for e in exps]
            probs_b = [p.astype(BF16) for p in probs]
            attended = [collect(tn(p, v)) for p, v in zip(probs_b, values)]
            dam = []
            for s, a in zip(ids, attended):
                gate = gate_scr[s, mine_rows, :]
                gy = gy_scr[s, mine_rows, :]
                gated_scr[s, mine_rows, :] = (gate * a).astype(BF16)
                dg_scr[s, mine_rows, :] = (gy * a * gate * (1.0 - gate)).astype(BF16)
                dam.append(spread((gy * gate).astype(BF16)))
            dprobs = [nt(v, d) for v, d in zip(values, dam)]
            ds = [
                p * (d - jnp.sum(p * d, axis=0, keepdims=True)) for p, d in zip(probs, dprobs)
            ]
            ds_b = [d.astype(BF16) for d in ds]
            total = ds[0]
            for d in ds[1:]:
                total = total + d
            ds_scr[...] += total
            for i, s in enumerate(ids):
                dq_scr[s, mine_rows, :] = (collect(tn(ds_b[i], keys[i])) * scale).astype(BF16)
            for i, s in enumerate(ids):
                dk_scr[s, key_rows, :] += nn(ds_b[i], qm[i])
                dv_scr[s, key_rows, :] += nn(probs_b[i], dam[i])
            return inner

        lax.fori_loop(0, samples // together, group, 0)
        total = ds_scr[...]
        tok_scr[...] += jnp.where(same, total, 0.0)
        pw_scr[...] += nn(pair_ref[w], total.astype(BF16))
        turned = total.T
        half = rows // 2
        for h in range(heads):
            low = turned[h * rows : h * rows + half]
            high = turned[h * rows + half : (h + 1) * rows]
            mine_ref[w, h * half : (h + 1) * half, :] = jnp.where(first_mine, low, high)
            theirs_ref[w, h * half : (h + 1) * half, :] = jnp.where(
                first_mine, high, low
            ).astype(BF16)
        return carry

    lax.fori_loop(0, windows, window, 0)

    sums_ref[...] = jnp.zeros_like(sums_ref)

    def finish(s, carry):
        dk = (dk_scr[s] * scale).astype(BF16)
        dv = dv_scr[s].astype(BF16)
        dq = dq_scr[s]
        dg = dg_scr[s]
        from_kv = nt(dk, wk_ref[...]) + nt(dv, wv_ref[...])
        to_lower_ref[s] = from_kv[0:halo].astype(BF16)
        to_upper_ref[s] = from_kv[halo + atoms : wide].astype(BF16)
        ga_ref[s] = from_kv[halo : halo + atoms] + nt(dq, wq_ref[...]) + nt(dg, wg_ref[...])
        own = act_ref[s]
        full = wide_act[s]
        c = channels
        sums_ref[0:c, :] += tn(own, dq)
        sums_ref[c : 2 * c, :] += tn(full, dk)
        sums_ref[2 * c : 3 * c, :] += tn(full, dv)
        sums_ref[3 * c : 4 * c, :] += tn(own, dg)
        sums_ref[4 * c : 5 * c, :] += tn(gated_scr[s], grad_ref[s])
        return carry

    lax.fori_loop(0, samples, finish, 0)
    shape = pw_scr.shape
    at_row = lax.broadcasted_iota(jnp.int32, shape, 0) // pair_channels
    at_col = lax.broadcasted_iota(jnp.int32, shape, 1) % rows
    diagonal = jnp.where(at_row == at_col, pw_scr[...], 0.0)
    base = 5 * channels
    sums_ref[base : base + pair_channels, :] = jnp.sum(
        diagonal.reshape(rows, pair_channels, stack), axis=0
    )
    sums_ref[base + pair_channels : base + pair_channels + 1, :] = jnp.sum(
        tok_scr[...], axis=0, keepdims=True
    )


def greet(barrier, devices):
    for device in devices:
        pl.semaphore_signal(
            barrier, inc=1, device_id=device, device_id_type=pl.DeviceIdType.MESH
        )


def remote(src, dst, sems, slot, device):
    return pltpu.make_async_remote_copy(
        src_ref=src,
        dst_ref=dst,
        send_sem=sems.at[0, slot],
        recv_sem=sems.at[1, slot],
        device_id=device,
        device_id_type=pl.DeviceIdType.MESH,
    )


def halo_kernel(
    ranges,
    span,
    act_ref,
    code_ref,
    before_ref,
    after_ref,
    code_before_ref,
    code_after_ref,
    sems,
):
    me = lax.axis_index("atoms")
    atoms = act_ref.shape[1]
    has_lower, has_upper = me > 0, me < ranges - 1
    lower, upper = {"atoms": me - 1}, {"atoms": me + 1}
    barrier = pltpu.get_barrier_semaphore()

    @pl.when(has_lower)
    def _():
        greet(barrier, [lower])

    @pl.when(has_upper)
    def _():
        greet(barrier, [upper])

    inside = jnp.logical_and(has_lower, has_upper)

    @pl.when(inside)
    def _():
        pl.semaphore_wait(barrier, 2)

    @pl.when(jnp.logical_not(inside))
    def _():
        pl.semaphore_wait(barrier, 1)

    last = code_ref.shape[0] - 1
    to_upper = [
        remote(act_ref.at[:, pl.ds(atoms - span, span)], before_ref, sems, 0, upper),
        remote(code_ref.at[pl.ds(last, 1)], code_before_ref, sems, 1, upper),
    ]
    to_lower = [
        remote(act_ref.at[:, pl.ds(0, span)], after_ref, sems, 2, lower),
        remote(code_ref.at[pl.ds(0, 1)], code_after_ref, sems, 3, lower),
    ]

    @pl.when(has_upper)
    def _():
        for copy in to_upper:
            copy.start()

    @pl.when(has_lower)
    def _():
        for copy in to_lower:
            copy.start()

    @pl.when(jnp.logical_not(has_lower))
    def _():
        before_ref[...] = jnp.zeros_like(before_ref)
        code_before_ref[...] = jnp.zeros_like(code_before_ref)

    @pl.when(jnp.logical_not(has_upper))
    def _():
        after_ref[...] = jnp.zeros_like(after_ref)
        code_after_ref[...] = jnp.zeros_like(code_after_ref)

    @pl.when(has_upper)
    def _():
        for copy in to_upper:
            copy.wait_send()
        for copy in to_lower:
            copy.wait_recv()

    @pl.when(has_lower)
    def _():
        for copy in to_lower:
            copy.wait_send()
        for copy in to_upper:
            copy.wait_recv()


def exchange_kernel(
    ranges,
    ga_ref,
    to_lower_ref,
    to_upper_ref,
    mine_ref,
    theirs_ref,
    sums_ref,
    wpair_ref,
    out_ref,
    pair_out_ref,
    total_ref,
    from_lower,
    from_upper,
    got,
    got_half,
    part,
    slots,
    wpair_scr,
    edge_sems,
    core_sems,
    scatter_sems,
    gather_sems,
):
    me = lax.axis_index("atoms")
    core = lax.axis_index("samples")
    other = 1 - core
    samples, atoms, channels = ga_ref.shape
    span = to_lower_ref.shape[1]
    chunk = part.shape[1]
    half = ranges * chunk
    has_lower, has_upper = me > 0, me < ranges - 1
    lower, upper, peer = {"atoms": me - 1}, {"atoms": me + 1}, {"samples": other}
    everyone = [{"atoms": lax.rem(me + d, ranges)} for d in range(1, ranges)]
    barrier = pltpu.get_barrier_semaphore()
    greet(barrier, [peer] + everyone)
    pl.semaphore_wait(barrier, ranges)

    half_copy = remote(
        sums_ref.at[pl.ds(pl.multiple_of(other * half, 8), half)], got_half, core_sems, 0, peer
    )
    half_copy.start()
    pair_copy = remote(theirs_ref, got, core_sems, 1, peer)
    pair_copy.start()
    up_copy = remote(to_upper_ref, from_lower, edge_sems, 0, upper)
    down_copy = remote(to_lower_ref, from_upper, edge_sems, 1, lower)

    @pl.when(has_upper)
    def _():
        up_copy.start()

    @pl.when(has_lower)
    def _():
        down_copy.start()

    half_copy.wait_recv()
    own_half = pl.ds(pl.multiple_of(core * half, 8), half)
    part[...] = (sums_ref[own_half, :] + got_half[...]).reshape(part.shape)
    scatter = []
    for d in range(1, ranges):
        target = lax.rem(me + d, ranges)
        copy = remote(part.at[target], slots.at[d - 1], scatter_sems, d - 1, everyone[d - 1])
        copy.start()
        scatter.append(copy)

    pair_channels, heads = wpair_ref.shape
    rows = mine_ref.shape[1] // heads
    stack = heads * rows
    lane = lax.broadcasted_iota(jnp.int32, (pair_channels, stack), 1)
    values = wpair_ref[...].astype(F32)
    wpair_rows = jnp.zeros((pair_channels, stack), F32)
    for h in range(heads):
        wpair_rows = jnp.where(lane // rows == h, values[:, h : h + 1], wpair_rows)
    for i in range(rows):
        wpair_scr[i * pair_channels : (i + 1) * pair_channels, :] = jnp.where(
            lane % rows == i, wpair_rows, 0.0
        ).astype(BF16)

    for copy in scatter:
        copy.wait_recv()
    chunk_total = part[me]
    for d in range(1, ranges):
        chunk_total = chunk_total + slots[d - 1]
    place = pl.ds(pl.multiple_of(core * half + me * chunk, 8), chunk)
    total_ref[place, :] = chunk_total
    gather = []
    for d in range(1, ranges):
        copy = remote(
            total_ref.at[place], total_ref.at[place], gather_sems, d - 1, everyone[d - 1]
        )
        copy.start()
        gather.append(copy)

    pair_copy.wait_recv()

    def one_window(w, carry):
        both = mine_ref[w] + got[w].astype(F32)
        high = both.astype(BF16)
        low = (both - high.astype(F32)).astype(BF16)
        weight = wpair_scr[...]
        pair_out_ref[w] = (nn(weight, high) + nn(weight, low)).astype(BF16)
        return carry

    lax.fori_loop(0, mine_ref.shape[0], one_window, 0)

    for copy in gather:
        copy.wait_recv()
    last_copy = remote(
        total_ref.at[own_half], total_ref.at[own_half], core_sems, 2, peer
    )
    last_copy.start()

    @pl.when(has_lower)
    def _():
        down_copy.wait_send()
        up_copy.wait_recv()

    @pl.when(has_upper)
    def _():
        up_copy.wait_send()
        down_copy.wait_recv()

    @pl.when(jnp.logical_not(has_lower))
    def _():
        from_lower[...] = jnp.zeros_like(from_lower)

    @pl.when(jnp.logical_not(has_upper))
    def _():
        from_upper[...] = jnp.zeros_like(from_upper)

    def one_sample(s, carry):
        out_ref[s, 0:span, :] = (ga_ref[s, 0:span, :] + from_lower[s].astype(F32)).astype(BF16)
        out_ref[s, span : atoms - span, :] = ga_ref[s, span : atoms - span, :].astype(BF16)
        out_ref[s, atoms - span : atoms, :] = (
            ga_ref[s, atoms - span : atoms, :] + from_upper[s].astype(F32)
        ).astype(BF16)
        return carry

    lax.fori_loop(0, samples, one_sample, 0)
    half_copy.wait_send()
    pair_copy.wait_send()
    for copy in scatter + gather:
        copy.wait_send()
    last_copy.wait()


def per_device(
    act,
    grad_out,
    pair,
    w_query,
    w_key,
    w_value,
    w_gate,
    w_out,
    w_pair,
    w_token,
    offsets,
    atom_token,
    padding,
):
    samples, atoms, channels = act.shape
    windows = offsets.shape[0]
    rows = atoms // windows
    pair_channels, heads = w_pair.shape
    span = pair.shape[-1]
    stack = heads * rows
    half = rows // 2
    ranges = lax.axis_size("atoms")
    wide = atoms + 2 * span
    vmem = pl.BlockSpec(memory_space=pltpu.VMEM)
    smem = pl.BlockSpec(memory_space=pltpu.SMEM)
    anywhere = pl.BlockSpec(memory_space=pl.ANY)
    position = jnp.arange(atoms, dtype=jnp.int32)
    codes = jnp.where(position < atoms - padding[0], atom_token + 1, 0)
    codes = codes.reshape(atoms // span, 1, span)
    query_code = jnp.tile((atom_token + 1).reshape(windows, 1, rows), (1, 1, heads))

    def first_kernel(*refs):
        halo_kernel(ranges, span, *refs)

    before, after, code_before, code_after = pl.pallas_call(
        first_kernel,
        out_shape=(
            jax.ShapeDtypeStruct((samples, span, channels), BF16),
            jax.ShapeDtypeStruct((samples, span, channels), BF16),
            jax.ShapeDtypeStruct((1, 1, span), jnp.int32),
            jax.ShapeDtypeStruct((1, 1, span), jnp.int32),
        ),
        in_specs=[pl.BlockSpec(memory_space=pl.ANY), vmem],
        out_specs=(vmem,) * 4,
        scratch_shapes=[pltpu.SemaphoreType.DMA((2, 4))],
        compiler_params=pltpu.CompilerParams(collective_id=0, has_side_effects=True),
        name="halo",
    )(act, codes)

    together = 8 if samples % 8 == 0 else 1
    chunk = 8 * pl.cdiv(5 * channels + pair_channels + 1, 16 * ranges)
    sum_rows = 2 * ranges * chunk

    def kernel(*refs):
        attention_kernel(heads, together, *refs)

    ga, to_lower, to_upper, mine, theirs, sums = pl.pallas_call(
        kernel,
        out_shape=(
            jax.ShapeDtypeStruct((samples, atoms, channels), F32),
            jax.ShapeDtypeStruct((samples, span, channels), BF16),
            jax.ShapeDtypeStruct((samples, span, channels), BF16),
            jax.ShapeDtypeStruct((windows, heads * half, span), F32),
            jax.ShapeDtypeStruct((windows, heads * half, span), BF16),
            jax.ShapeDtypeStruct((sum_rows, channels), F32),
        ),
        in_specs=[smem, smem] + [vmem] * 15,
        out_specs=(vmem,) * 6,
        scratch_shapes=[
            pltpu.VMEM((samples, wide, channels), BF16),
            pltpu.VMEM((samples, wide, channels), F32),
            pltpu.VMEM((samples, wide, channels), F32),
            pltpu.VMEM((samples, wide, channels), F32),
            pltpu.VMEM((samples, wide, channels), F32),
            pltpu.VMEM((samples, atoms, channels), BF16),
            pltpu.VMEM((samples, atoms, channels), F32),
            pltpu.VMEM((samples, atoms, channels), F32),
            pltpu.VMEM((samples, atoms, channels), BF16),
            pltpu.VMEM((samples, atoms, channels), BF16),
            pltpu.VMEM((samples, atoms, channels), BF16),
            pltpu.VMEM((rows * pair_channels, stack), F32),
            pltpu.VMEM((span, stack), F32),
            pltpu.VMEM((span, stack), F32),
            pltpu.VMEM((span, stack), F32),
            pltpu.VMEM((wide, stack), F32),
            pltpu.VMEM((rows * pair_channels, stack), BF16),
        ],
        compiler_params=pltpu.CompilerParams(vmem_limit_bytes=56 * 1024 * 1024),
        name="attention",
    )(
        offsets,
        w_token,
        act,
        before,
        after,
        grad_out,
        pair.reshape(windows, rows * pair_channels, span),
        w_query,
        w_key,
        w_value,
        w_gate,
        w_out,
        w_pair,
        codes,
        code_before,
        code_after,
        query_code,
    )

    def last_kernel(*refs):
        exchange_kernel(ranges, *refs)

    edge = pltpu.VMEM((samples, span, channels), BF16)
    grad_act, grad_pair, total = pl.pallas_call(
        last_kernel,
        out_shape=(
            jax.ShapeDtypeStruct((samples, atoms, channels), BF16),
            jax.ShapeDtypeStruct((windows, half * pair_channels, span), BF16),
            jax.ShapeDtypeStruct((sum_rows, channels), F32),
        ),
        in_specs=[vmem, anywhere, anywhere, vmem, anywhere, vmem, vmem],
        out_specs=(vmem,) * 3,
        scratch_shapes=[
            edge,
            edge,
            pltpu.VMEM((windows, heads * half, span), BF16),
            pltpu.VMEM((ranges * chunk, channels), F32),
            pltpu.VMEM((ranges, chunk, channels), F32),
            pltpu.VMEM((ranges - 1, chunk, channels), F32),
            pltpu.VMEM((half * pair_channels, heads * half), BF16),
            pltpu.SemaphoreType.DMA((2, 2)),
            pltpu.SemaphoreType.DMA((2, 3)),
            pltpu.SemaphoreType.DMA((2, ranges - 1)),
            pltpu.SemaphoreType.DMA((2, ranges - 1)),
        ],
        compiler_params=pltpu.CompilerParams(
            collective_id=1, has_side_effects=True, vmem_limit_bytes=40 * 1024 * 1024
        ),
        name="exchange",
    )(ga, to_lower, to_upper, mine, theirs, sums, w_pair)

    base = 5 * channels
    grad_weights = total[:base].reshape(5, channels, channels)
    grad_pair_weight = jnp.sum(
        total[base : base + pair_channels].reshape(pair_channels, heads, rows), axis=-1
    )
    grad_token_weight = jnp.sum(total[base + pair_channels].reshape(heads, rows), axis=-1)
    grad_pair = grad_pair.reshape(windows, half, pair_channels, span)
    return (grad_act, grad_pair, grad_weights, grad_pair_weight, grad_token_weight)


def solution(mesh):
    in_specs = (
        P("samples", ("groups", "atoms"), None),
        P("samples", ("groups", "atoms"), None),
        P(("groups", "atoms"), None, None, None),
        P(),
        P(),
        P(),
        P(),
        P(),
        P(),
        P(),
        P(("groups", "atoms")),
        P(("groups", "atoms")),
        P(("groups", "atoms")),
    )
    out_specs = (
        P("samples", ("groups", "atoms"), None),
        P(("groups", "atoms"), "samples", None, None),
        P("groups", None, None),
        P("groups", None),
        P("groups"),
    )
    return jax.shard_map(
        per_device, mesh=mesh, in_specs=in_specs, out_specs=out_specs, check_vma=False
    )
```
